768 devices in a mesh: grp: 48 (over z, x), blk: 16 (over y, core).
Axes of the slice: x: 4, y: 8, z: 12, core: 2. Of those that a mesh axis runs over, the one named last changes fastest.
Arguments:
- grad_final: bfloat16 [786432, 128], P(('grp', 'blk')), may hold values from -8 to 8
- local_tiles: bfloat16 [6144, 8, 128, 128], P(('grp', 'blk')), may hold values from 0 to 0.67103634, as said below
- local_source: int32 [6144, 8], P(('grp', 'blk')), may hold values from 0 to 7
- near_tiles: bfloat16 [48, 16, 2, 128, 128], P('grp', 'blk'), may hold values from 0 to 0.67103634, as said below
- near_source: int32 [48, 16, 2], P('grp', 'blk'), may hold values from 0 to 7
- near_target: int32 [48, 16, 2], P('grp', 'blk'), may hold values from 0 to 7
- line_tiles: bfloat16 [48, 16, 16, 128, 128], P('grp', 'blk'), may hold values from 0 to 0.67103634, as said below
- line_source: int32 [48, 16, 16], P('grp', 'blk'), may hold values from 0 to 7
- line_target: int32 [48, 16, 16], P('grp', 'blk'), may hold values from 0 to 7
- line_live: int32 [48, 16, 16], P('grp', 'blk'), may hold values 0 or 1
Outputs:
- grad_embed: float32 [786432, 128], P(('grp', 'blk'))
The draws below stay inside these ranges and needn't reach their ends.
Inputs may be any that keep to these rules, and one draw needn't show every extreme that they name: `local_tiles`: nonnegative tile weights. `near_tiles`: nonnegative tile weights. `line_tiles`: nonnegative tile weights. `local_source`: block numbers among the 8 blocks of one device. `near_source`: block numbers among the 8 blocks of one device. `near_target`: block numbers among the 8 blocks of one device. `line_source`: block numbers among the 8 blocks of one device. `line_target`: block numbers among the 8 blocks of one device.
All inputs are finite; a program needn't handle non-finite values. No bound on the sum of `line_live` on one device may be relied on, other than what follows from the above.
Results may differ from the reference program's by a relative error of at most 0.0027.
Values may be sent and summed in bfloat16 or wider, within the bound.
No kernel may reach another device: no remote copies, remote signals or barrier semaphores. Data moves between devices by JAX's collectives and lax.ppermute only.
A program may use at most 32 MiB of HBM per device.

```python
import math
import jax
import jax.numpy as jnp
from jax import lax

EMB = 128
TILE = 128
NBLK = 8
LOC_K = 8
LAYERS = 3
NLOC = 6144
NROWS = 786432
N_GRP = 48
N_BLK = 16


def tile_law(key, shape):
    leading = shape[:-2]
    scale_key = jax.random.fold_in(key, 11)
    entry_key = jax.random.fold_in(key, 12)
    exponent = 64.0
    weight_moment = (16.0 - 0.0625) / (2.0 * math.log(16.0))
    base_scale = 0.8 * math.sqrt(2.0 * exponent + 1.0) / math.sqrt(weight_moment * TILE * (LOC_K + 2))
    weight = jnp.exp(jax.random.uniform(scale_key, leading + (1, 1), jnp.float32, math.log(0.25), math.log(4.0)))
    unit_draw = jax.random.uniform(entry_key, shape, jnp.float32, 0.0, 1.0)
    entries = jnp.power(unit_draw, exponent)
    return (base_scale * weight * entries).astype(jnp.bfloat16)


def draw_local_tiles(key, part):
    return tile_law(key, (NLOC, LOC_K, TILE, TILE))


def draw_near_tiles(key, part):
    return tile_law(key, (N_GRP, N_BLK, 2, TILE, TILE))


def draw_line_tiles(key, part):
    return tile_law(key, (N_GRP, N_BLK, N_BLK, TILE, TILE))


def draw_grad_final(key, part):
    scale_key = jax.random.fold_in(key, 22)
    jitter_key = jax.random.fold_in(key, 23)
    row_scale = jax.random.uniform(scale_key, (NROWS, 1), jnp.float32, 0.5, 2.0)
    jitter = jnp.clip(jax.random.normal(jitter_key, (NROWS, EMB), jnp.float32), -4.0, 4.0)
    return (row_scale * jitter).astype(jnp.bfloat16)


def touch_ends(values, key, least, high):
    place = [jax.random.randint(jax.random.fold_in(key, axis), (), 0, length) for axis, length in enumerate(values.shape)]
    longest = values.shape.index(max(values.shape))
    neighbour = place[:longest] + [(place[longest] + 1) % values.shape[longest]] + place[longest + 1:]
    return values.at[tuple(place)].set(least).at[tuple(neighbour)].set(high)


def setup_inputs(seed: int = 0) -> dict:
    splits = jax.random.split(jax.random.key(seed), 11)
    return {
        "grad_final": draw_grad_final(jax.random.fold_in(splits[10], 71), 0),
        "local_tiles": draw_local_tiles(jax.random.fold_in(splits[10], 71), 0),
        "local_source": touch_ends(jax.random.randint(splits[2], (NLOC, LOC_K), 0, NBLK), jax.random.fold_in(splits[2], 1), 0, NBLK - 1).astype(jnp.int32),
        "near_tiles": draw_near_tiles(jax.random.fold_in(splits[10], 71), 0),
        "near_source": touch_ends(jax.random.randint(splits[4], (N_GRP, N_BLK, 2), 0, NBLK), jax.random.fold_in(splits[4], 1), 0, NBLK - 1).astype(jnp.int32),
        "near_target": touch_ends(jax.random.randint(splits[5], (N_GRP, N_BLK, 2), 0, NBLK), jax.random.fold_in(splits[5], 1), 0, NBLK - 1).astype(jnp.int32),
        "line_tiles": draw_line_tiles(jax.random.fold_in(splits[10], 71), 0),
        "line_source": touch_ends(jax.random.randint(splits[7], (N_GRP, N_BLK, N_BLK), 0, NBLK), jax.random.fold_in(splits[7], 1), 0, NBLK - 1).astype(jnp.int32),
        "line_target": touch_ends(jax.random.randint(splits[8], (N_GRP, N_BLK, N_BLK), 0, NBLK), jax.random.fold_in(splits[8], 1), 0, NBLK - 1).astype(jnp.int32),
        "line_live": touch_ends((jax.random.randint(splits[9], (N_GRP, N_BLK, N_BLK), 0, 4) < 3).astype(jnp.int32), jax.random.fold_in(splits[9], 1), 0, 1),
    }


def propagate(grad_state, tiles_by_dev, source_by_dev, near_tiles, near_source, near_target, line_tiles, line_source, line_target, line_live):
    grp_count = N_GRP
    blk_count = N_BLK
    blk_iota = jnp.arange(blk_count)

    def per_group(group_index):
        group_state = grad_state[group_index]
        group_tiles = tiles_by_dev[group_index].astype(jnp.float32)
        group_source = source_by_dev[group_index]
        picked = group_state[blk_iota[:, None, None], group_source].astype(jnp.float32)
        local_part = jnp.einsum("nbkrc,nbkrf->nbcf", group_tiles, picked)
        near_pick = group_state[blk_iota[:, None], near_source[group_index]].astype(jnp.float32)
        near_send = jnp.einsum("nsrc,nsrf->nscf", near_tiles[group_index].astype(jnp.float32), near_pick).astype(jnp.bfloat16)
        line_pick = group_state[blk_iota[:, None], line_source[group_index]].astype(jnp.float32)
        line_prod = jnp.einsum("nsrc,nsrf->nscf", line_tiles[group_index].astype(jnp.float32), line_pick)
        line_send = (line_prod * line_live[group_index][:, :, None, None].astype(jnp.float32)).astype(jnp.bfloat16)
        return local_part, near_send, line_send

    local_part, near_send, line_send = lax.map(per_group, jnp.arange(grp_count))
    full_shape = (grp_count, blk_count, blk_count)
    grp_index = jnp.broadcast_to(jnp.arange(grp_count)[:, None, None], full_shape)
    blk_target = jnp.broadcast_to(jnp.arange(blk_count)[None, None, :], full_shape)
    accumulated = local_part.at[grp_index, blk_target, line_target].add(line_send.astype(jnp.float32))
    for slot_index in range(2):
        target_grp = jnp.arange(grp_count) + 2 * slot_index - 1
        valid_mask = ((target_grp >= 0) & (target_grp < grp_count)).astype(jnp.float32)
        target_grp = jnp.clip(target_grp, 0, grp_count - 1)
        near_vals = near_send[:, :, slot_index].astype(jnp.float32) * valid_mask[:, None, None, None]
        pair_shape = (grp_count, blk_count)
        accumulated = accumulated.at[
            jnp.broadcast_to(target_grp[:, None], pair_shape),
            jnp.broadcast_to(jnp.arange(blk_count)[None, :], pair_shape),
            near_target[:, :, slot_index],
        ].add(near_vals)
    return accumulated.astype(jnp.bfloat16)


def reference(grad_final, local_tiles, local_source, near_tiles, near_source, near_target, line_tiles, line_source, line_target, line_live):
    grad_state = grad_final.reshape(N_GRP, N_BLK, NBLK, TILE, EMB)
    tiles_by_dev = local_tiles.reshape(N_GRP, N_BLK, NBLK, LOC_K, TILE, TILE)
    source_by_dev = local_source.reshape(N_GRP, N_BLK, NBLK, LOC_K)
    running_sum = grad_final.astype(jnp.float32)
    for layer_index in range(LAYERS):
        grad_state = propagate(grad_state, tiles_by_dev, source_by_dev, near_tiles, near_source, near_target, line_tiles, line_source, line_target, line_live)
        running_sum = running_sum + grad_state.reshape(NROWS, EMB).astype(jnp.float32)
    return running_sum / (LAYERS + 1)
```

```python
import jax
import jax.numpy as jnp
from jax import lax
from jax.experimental import pallas as pl
from jax.experimental.pallas import tpu as pltpu
from jax.sharding import PartitionSpec as P

LAYERS = 3
ID_ROWS = 8

VMEM = pl.BlockSpec(memory_space=pltpu.VMEM)
SMEM = pl.BlockSpec(memory_space=pltpu.SMEM)
HBM = pl.BlockSpec(memory_space=pltpu.HBM)
PARAMS = pltpu.CompilerParams(vmem_limit_bytes=8 * 2**20)


def on_chip(*arrays):
    return [pltpu.with_memory_space_constraint(array, pltpu.VMEM) for array in arrays]


def off_chip(*arrays):
    return [pltpu.with_memory_space_constraint(array, pltpu.HBM) for array in arrays]


def shifted(value, axis, steps):
    count = lax.axis_size(axis)
    leading, last = (max(0, -steps), min(count, count - steps))
    return lax.ppermute(value, axis, [(source, source + steps) for source in range(leading, last)])


def dot32(left, right):
    return jnp.dot(left, right, preferred_element_type=jnp.float32)


def id_rows(block_id, width):
    return jnp.full((ID_ROWS, width), block_id).astype(jnp.float32).astype(jnp.bfloat16)


def read_id(rows):
    return jnp.max(rows.astype(jnp.float32)).astype(jnp.int32)


def line_products(state, tiles, source, live, terms, products, sent, ready=None, target=None):
    slots, emb = terms.shape[0], state.shape[1]
    for slot in range(slots):
        if ready is not None:
            ready(slot)
        product = dot32(state[source[0, 0, slot]], tiles[slot])
        products[slot, :emb] = (product * live[0, 0, slot].astype(jnp.float32)).astype(products.dtype)
        if target is not None:
            products[slot, emb:] = id_rows(target[0, 0, slot], products.shape[2])
        pltpu.make_async_copy(products.at[slot], terms.at[slot], sent.at[slot]).start()


def wait_sent(products, terms, sent):
    for slot in range(terms.shape[0]):
        pltpu.make_async_copy(products.at[slot], terms.at[slot], sent.at[slot]).wait()


def first_kernel(
    grad, line_tiles, near_tiles, line_from, line_live, line_to, near_from, near_to,
    state, terms, near_down, near_up,
    grad_in, line_in, near_in, products, sent, got,
):
    slots, blocks, emb = terms.shape[0], state.shape[0], state.shape[1]
    grad_copy = pltpu.make_async_copy(grad, grad_in, got.at[slots])
    near_copy = pltpu.make_async_copy(near_tiles.at[0, 0], near_in, got.at[slots + 1])
    line_copies = [
        pltpu.make_async_copy(line_tiles.at[0, 0, slot], line_in.at[slot], got.at[slot]) for slot in range(slots)
    ]
    grad_copy.start()
    for copy in line_copies:
        copy.start()
    near_copy.start()
    grad_copy.wait()
    for block in range(blocks):
        state[block] = grad_in[block].T
    line_products(
        state, line_in, line_from, line_live, terms, products, sent,
        ready=lambda slot: line_copies[slot].wait(), target=line_to,
    )
    near_copy.wait()
    for slot, near in enumerate((near_down, near_up)):
        near[:emb] = dot32(state[near_from[0, 0, slot]], near_in[slot]).astype(near.dtype)
        near[emb:] = id_rows(near_to[0, 0, slot], near.shape[1])
    wait_sent(products, terms, sent)


def local_blocks(state, tiles, source, local, tiles_in, got, after=None):
    blocks, per_block, rows, cols = tiles.shape
    copies = [pltpu.make_async_copy(tiles.at[block], tiles_in.at[block], got.at[block]) for block in range(blocks)]
    for copy in copies:
        copy.start()
    for block in range(blocks):
        left = jnp.concatenate([state[source[block, k]] for k in range(per_block)], axis=1)
        copies[block].wait()
        local[block] = dot32(left, tiles_in[block].reshape(per_block * rows, cols))


def local_kernel(state, tiles, source, local, tiles_in, got):
    local_blocks(state, tiles, source, local, tiles_in, got)


def last_local_kernel(state, tiles, source, grad, earlier, local, running, tiles_in, got):
    local_blocks(state, tiles, source, local, tiles_in, got)
    for block in range(state.shape[0]):
        running[block] = (
            grad[block].astype(jnp.float32)
            + earlier[block].T.astype(jnp.float32)
            + state[block].T.astype(jnp.float32)
        )


def collect(ids, line_got, local, nears, total):
    slots, emb = line_got.shape[0], local.shape[1]
    total[...] = local[...]
    for index, near in enumerate(nears):
        target = ids[slots + index]
        total[target] = total[target] + near[:emb].astype(jnp.float32)
    for slot in range(slots):
        target = ids[slot]
        total[target] = total[target] + line_got[slot, :emb].astype(jnp.float32)


def next_kernel(
    *refs, first
):
    if first:
        line_got, local, from_below, from_above, *refs = refs
    else:
        ids, line_got, local, from_below, from_above, *refs = refs
    line_tiles, near_tiles, line_from, line_live, near_from, *refs = refs
    if first:
        state, terms, near_down, near_up, ids, *refs = refs
    else:
        state, terms, near_down, near_up, *refs = refs
    total, products, sent = refs
    slots, emb = terms.shape[0], state.shape[1]
    if first:
        for slot in range(slots):
            ids[slot] = read_id(line_got[slot, emb:])
        for index, near in enumerate((from_below, from_above)):
            ids[slots + index] = read_id(near[emb:])
    collect(ids, line_got, local, (from_below, from_above), total)
    state[...] = total[...].astype(state.dtype)
    line_products(state, line_tiles.at[0, 0], line_from, line_live, terms, products, sent)
    for slot, near in enumerate((near_down, near_up)):
        near[...] = dot32(state[near_from[0, 0, slot]], near_tiles[0, 0, slot]).astype(near.dtype)
    wait_sent(products, terms, sent)


def last_kernel(ids, line_got, local, from_below, from_above, running, out, total, final, sent):
    collect(ids, line_got, local, (from_below, from_above), total)
    copies = [pltpu.make_async_copy(final.at[block], out.at[block], sent.at[block]) for block in range(out.shape[0])]
    for block, copy in enumerate(copies):
        newest = total[block].astype(jnp.bfloat16).T.astype(jnp.float32)
        final[block] = (running[block] + newest) * (1.0 / (LAYERS + 1))
        copy.start()
    for copy in copies:
        copy.wait()


def on_device(
    grad_final, local_tiles, local_source, near_tiles, near_source, near_target,
    line_tiles, line_source, line_target, line_live,
):
    blocks, per_block, rows, cols = local_tiles.shape
    emb = grad_final.shape[1]
    slots = line_tiles.shape[2]
    nears = near_tiles.shape[2]
    bf16, f32 = jnp.bfloat16, jnp.float32
    dma = pltpu.SemaphoreType.DMA
    grad = grad_final.reshape(blocks, rows, emb)
    state_shape = pltpu.VMEM((blocks, emb, rows), bf16)
    sum_shape = pltpu.VMEM((blocks, emb, rows), f32)

    def emitted(extra):
        near = pltpu.VMEM((emb + extra, cols), bf16)
        terms = (slots, emb + extra, cols)
        return (
            (state_shape, pltpu.HBM(terms, bf16), near, near),
            (VMEM, HBM, VMEM, VMEM),
            [pltpu.VMEM(terms, bf16), dma((slots,))],
        )

    total = pltpu.VMEM((blocks, emb, rows), f32)
    local_scratch = [pltpu.VMEM(local_tiles.shape, bf16), dma((blocks,))]
    (local_tiles,) = off_chip(local_tiles)

    shapes, specs, staging = emitted(ID_ROWS)
    state, terms, near_down, near_up = pl.pallas_call(
        first_kernel,
        out_shape=shapes,
        in_specs=[HBM] * 3 + [SMEM] * 5,
        out_specs=specs,
        scratch_shapes=[
            pltpu.VMEM((blocks, rows, emb), bf16),
            pltpu.VMEM((slots, rows, cols), bf16),
            pltpu.VMEM((nears, rows, cols), bf16),
            *staging,
            dma((slots + 2,)),
        ],
        compiler_params=PARAMS,
        name="first_terms",
    )(*off_chip(grad, line_tiles, near_tiles, line_source, line_live, line_target, near_source, near_target))
    line_tiles, near_tiles = on_chip(line_tiles, near_tiles)
    states, ids = [state], None
    for layer in range(LAYERS):
        line_got = lax.all_to_all(terms, "blk", split_axis=0, concat_axis=0, tiled=True)
        from_below = shifted(near_up, "grp", 1)
        from_above = shifted(near_down, "grp", -1)
        line_got, from_below, from_above, state = on_chip(line_got, from_below, from_above, state)
        if layer < LAYERS - 1:
            local = pl.pallas_call(
                local_kernel,
                out_shape=sum_shape,
                in_specs=[VMEM, HBM, SMEM],
                out_specs=VMEM,
                scratch_shapes=local_scratch,
                compiler_params=PARAMS,
                name="local_sums",
            )(state, local_tiles, local_source)
            first = layer == 0
            shapes, specs, staging = emitted(0)
            if first:
                shapes += (jax.ShapeDtypeStruct((slots + nears,), jnp.int32),)
                specs += (SMEM,)
            results = pl.pallas_call(
                lambda *refs, first=first: next_kernel(*refs, first=first),
                out_shape=shapes,
                in_specs=[SMEM] * (not first) + [VMEM] * 6 + [SMEM] * 3,
                out_specs=specs,
                scratch_shapes=[total, *staging],
                compiler_params=PARAMS,
                name="next_state",
            )(
                *(() if first else (ids,)), line_got, local, from_below, from_above,
                line_tiles, near_tiles, line_source, line_live, near_source,
            )
            state, terms, near_down, near_up = results[:4]
            ids = results[4] if first else ids
            states.append(state)
        else:
            local, running = pl.pallas_call(
                last_local_kernel,
                out_shape=(sum_shape, pltpu.VMEM((blocks, rows, emb), f32)),
                in_specs=[VMEM, HBM, SMEM, VMEM, VMEM],
                out_specs=(VMEM, VMEM),
                scratch_shapes=local_scratch,
                compiler_params=PARAMS,
                name="last_local_sums",
            )(state, local_tiles, local_source, grad, states[1])
            out = pl.pallas_call(
                last_kernel,
                out_shape=jax.ShapeDtypeStruct((blocks, rows, emb), f32),
                in_specs=[SMEM] + [VMEM] * 5,
                out_specs=HBM,
                scratch_shapes=[total, pltpu.VMEM((blocks, rows, emb), f32), dma((blocks,))],
                compiler_params=PARAMS,
                name="last_state",
            )(ids, line_got, local, from_below, from_above, running)
    return out.reshape(blocks * rows, emb)


def solution(mesh):
    return jax.shard_map(
        on_device,
        mesh=mesh,
        in_specs=(
            P(("grp", "blk"), None),
            P(("grp", "blk"), None, None, None),
            P(("grp", "blk"), None),
            P("grp", "blk", None, None, None),
            P("grp", "blk", None),
            P("grp", "blk", None),
            P("grp", "blk", None, None, None),
            P("grp", "blk", None),
            P("grp", "blk", None),
            P("grp", "blk", None),
        ),
        out_specs=P(("grp", "blk"), None),
        check_vma=False,
    )
```

```python
import jax
import jax.numpy as jnp
from jax import lax
from jax.experimental import pallas as pl
from jax.experimental.pallas import tpu as pltpu
from jax.sharding import PartitionSpec as P

LAYERS = 3
ID_ROWS = 8
SENT_CHUNK = 2
GOT_CHUNK = 16

VMEM = pl.BlockSpec(memory_space=pltpu.VMEM)
SMEM = pl.BlockSpec(memory_space=pltpu.SMEM)
HBM = pl.BlockSpec(memory_space=pltpu.HBM)
PARAMS = pltpu.CompilerParams(vmem_limit_bytes=8 * 2**20)


def on_chip(*arrays):
    return [pltpu.with_memory_space_constraint(array, pltpu.VMEM) for array in arrays]


def off_chip(*arrays):
    return [pltpu.with_memory_space_constraint(array, pltpu.HBM) for array in arrays]


def in_scalars(*arrays):
    return [pltpu.with_memory_space_constraint(array, pltpu.SMEM) for array in arrays]


def shifted(value, axis, steps):
    count = lax.axis_size(axis)
    leading, last = (max(0, -steps), min(count, count - steps))
    return lax.ppermute(value, axis, [(source, source + steps) for source in range(leading, last)])


def dot32(left, right):
    return jnp.dot(left, right, preferred_element_type=jnp.float32)


def id_rows(block_id, width):
    return jnp.full((ID_ROWS, width), block_id).astype(jnp.float32).astype(jnp.bfloat16)


def read_id(rows):
    return jnp.max(rows.astype(jnp.float32)).astype(jnp.int32)


def send_copies(products, terms, sent):
    return [
        pltpu.make_async_copy(products.at[pl.ds(start, SENT_CHUNK)], terms.at[pl.ds(start, SENT_CHUNK)], sent.at[start // SENT_CHUNK])
        for start in range(0, terms.shape[0], SENT_CHUNK)
    ]


def line_products(state, tiles, source, live, terms, products, sent, ready=None, target=None):
    slots, emb = terms.shape[0], state.shape[1]
    copies = send_copies(products, terms, sent)
    for slot in range(slots):
        if ready is not None and slot % GOT_CHUNK == 0:
            ready[slot // GOT_CHUNK].wait()
        product = dot32(state[source[0, 0, slot]], tiles[slot])
        products[slot, :emb] = (product * live[0, 0, slot].astype(jnp.float32)).astype(products.dtype)
        if target is not None:
            products[slot, emb:] = id_rows(target[0, 0, slot], products.shape[2])
        if slot % SENT_CHUNK == SENT_CHUNK - 1:
            copies[slot // SENT_CHUNK].start()


def wait_sent(products, terms, sent):
    for copy in send_copies(products, terms, sent):
        copy.wait()


def first_kernel(
    grad, line_tiles, near_tiles, line_from, line_live, near_from, source, line_to, near_to,
    state, terms, near_down, near_up, line_from_out, line_live_out, near_from_out, source_out,
    grad_in, line_in, near_in, line_to_in, near_to_in, products, sent, got, got_index,
):
    slots, blocks, emb = terms.shape[0], state.shape[0], state.shape[1]
    pairs = (
        (line_from, line_from_out), (line_live, line_live_out), (line_to, line_to_in),
        (near_from, near_from_out), (near_to, near_to_in), (source, source_out),
    )
    index_copies = [pltpu.make_async_copy(*pair, got_index.at[number]) for number, pair in enumerate(pairs)]
    half = blocks // 2
    grad_copies = [
        pltpu.make_async_copy(grad.at[pl.ds(start, half)], grad_in.at[pl.ds(start, half)], got.at[slots + start // half])
        for start in range(0, blocks, half)
    ]
    near_copy = pltpu.make_async_copy(near_tiles.at[0, 0], near_in, got.at[slots + 2])
    line_copies = [
        pltpu.make_async_copy(
            line_tiles.at[0, 0, pl.ds(start, GOT_CHUNK)], line_in.at[pl.ds(start, GOT_CHUNK)], got.at[start // GOT_CHUNK]
        )
        for start in range(0, slots, GOT_CHUNK)
    ]
    for copy in (*grad_copies, *index_copies, *line_copies, near_copy):
        copy.start()
    for block in range(blocks):
        if block % half == 0:
            grad_copies[block // half].wait()
        state[block] = grad_in[block].T
    for copy in index_copies[:3]:
        copy.wait()
    line_products(
        state, line_in, line_from_out, line_live_out, terms, products, sent,
        ready=line_copies, target=line_to_in,
    )
    for copy in (near_copy, *index_copies[3:]):
        copy.wait()
    for slot, near in enumerate((near_down, near_up)):
        near[:emb] = dot32(state[near_from_out[0, 0, slot]], near_in[slot]).astype(near.dtype)
        near[emb:] = id_rows(near_to_in[0, 0, slot], near.shape[1])
    wait_sent(products, terms, sent)


def local_blocks(state, tiles, source, local, tiles_in, got, after=None):
    blocks, per_block, rows, cols = tiles.shape
    copies = [pltpu.make_async_copy(tiles.at[block], tiles_in.at[block], got.at[block]) for block in range(blocks)]
    for copy in copies:
        copy.start()
    for block in range(blocks):
        left = jnp.concatenate([state[source[block, k]] for k in range(per_block)], axis=1)
        copies[block].wait()
        local[block] = dot32(left, tiles_in[block].reshape(per_block * rows, cols))


def local_kernel(state, tiles, source, local, tiles_in, got):
    local_blocks(state, tiles, source, local, tiles_in, got)


def last_local_kernel(state, tiles, source, grad, earlier, local, running, tiles_in, got):
    local_blocks(state, tiles, source, local, tiles_in, got)
    for block in range(state.shape[0]):
        running[block] = (
            grad[block].astype(jnp.float32)
            + earlier[block].T.astype(jnp.float32)
            + state[block].T.astype(jnp.float32)
        )


def collect(ids, line_got, local, nears, total):
    slots, emb = line_got.shape[0], local.shape[1]
    total[...] = local[...]
    for index, near in enumerate(nears):
        target = ids[slots + index]
        total[target] = total[target] + near[:emb].astype(jnp.float32)
    for slot in range(slots):
        target = ids[slot]
        total[target] = total[target] + line_got[slot, :emb].astype(jnp.float32)


def next_kernel(
    *refs, first
):
    if first:
        line_got, local, from_below, from_above, *refs = refs
    else:
        ids, line_got, local, from_below, from_above, *refs = refs
    line_tiles, near_tiles, line_from, line_live, near_from, *refs = refs
    if first:
        state, terms, near_down, near_up, ids, *refs = refs
    else:
        state, terms, near_down, near_up, *refs = refs
    total, products, sent = refs
    slots, emb = terms.shape[0], state.shape[1]
    if first:
        for slot in range(slots):
            ids[slot] = read_id(line_got[slot, emb:])
        for index, near in enumerate((from_below, from_above)):
            ids[slots + index] = read_id(near[emb:])
    collect(ids, line_got, local, (from_below, from_above), total)
    state[...] = total[...].astype(state.dtype)
    line_products(state, line_tiles.at[0, 0], line_from, line_live, terms, products, sent)
    for slot, near in enumerate((near_down, near_up)):
        near[...] = dot32(state[near_from[0, 0, slot]], near_tiles[0, 0, slot]).astype(near.dtype)
    wait_sent(products, terms, sent)


def last_kernel(ids, line_got, local, from_below, from_above, running, out, total, final, sent):
    collect(ids, line_got, local, (from_below, from_above), total)
    copies = [pltpu.make_async_copy(final.at[block], out.at[block], sent.at[block]) for block in range(out.shape[0])]
    for block, copy in enumerate(copies):
        newest = total[block].astype(jnp.bfloat16).T.astype(jnp.float32)
        final[block] = (running[block] + newest) * (1.0 / (LAYERS + 1))
        copy.start()
    for copy in copies:
        copy.wait()


def on_device(
    grad_final, local_tiles, local_source, near_tiles, near_source, near_target,
    line_tiles, line_source, line_target, line_live,
):
    blocks, per_block, rows, cols = local_tiles.shape
    emb = grad_final.shape[1]
    slots = line_tiles.shape[2]
    nears = near_tiles.shape[2]
    bf16, f32 = jnp.bfloat16, jnp.float32
    dma = pltpu.SemaphoreType.DMA
    grad = grad_final.reshape(blocks, rows, emb)
    state_shape = pltpu.VMEM((blocks, emb, rows), bf16)
    sum_shape = pltpu.VMEM((blocks, emb, rows), f32)

    def emitted(extra):
        near = pltpu.VMEM((emb + extra, cols), bf16)
        terms = (slots, emb + extra, cols)
        return (
            (state_shape, pltpu.HBM(terms, bf16), near, near),
            (VMEM, HBM, VMEM, VMEM),
            [pltpu.VMEM(terms, bf16), dma((slots,))],
        )

    total = pltpu.VMEM((blocks, emb, rows), f32)
    local_scratch = [pltpu.VMEM(local_tiles.shape, bf16), dma((blocks,))]
    (local_tiles,) = off_chip(local_tiles)

    indices = (line_source, line_live, near_source, local_source)
    shapes, specs, staging = emitted(ID_ROWS)
    state, terms, near_down, near_up, *indices = pl.pallas_call(
        first_kernel,
        out_shape=(*shapes, *(pltpu.SMEM(index.shape, jnp.int32) for index in indices)),
        in_specs=[HBM] * 9,
        out_specs=(*specs, *(SMEM for _ in indices)),
        scratch_shapes=[
            pltpu.VMEM((blocks, rows, emb), bf16),
            pltpu.VMEM((slots, rows, cols), bf16),
            pltpu.VMEM((nears, rows, cols), bf16),
            pltpu.SMEM(line_target.shape, jnp.int32),
            pltpu.SMEM(near_target.shape, jnp.int32),
            *staging,
            dma((slots + 3,)),
            dma((6,)),
        ],
        compiler_params=PARAMS,
        name="first_terms",
    )(*off_chip(grad, line_tiles, near_tiles, *indices, line_target, near_target))
    line_source, line_live, near_source, local_source = in_scalars(*indices)
    line_tiles, near_tiles = on_chip(line_tiles, near_tiles)
    states, ids = [state], None
    for layer in range(LAYERS):
        line_got = lax.all_to_all(terms, "blk", split_axis=0, concat_axis=0, tiled=True)
        from_below = shifted(near_up, "grp", 1)
        from_above = shifted(near_down, "grp", -1)
        line_got, from_below, from_above, state = on_chip(line_got, from_below, from_above, state)
        if layer < LAYERS - 1:
            local = pl.pallas_call(
                local_kernel,
                out_shape=sum_shape,
                in_specs=[VMEM, HBM, SMEM],
                out_specs=VMEM,
                scratch_shapes=local_scratch,
                compiler_params=PARAMS,
                name="local_sums",
            )(state, local_tiles, local_source)
            first = layer == 0
            shapes, specs, staging = emitted(0)
            if first:
                shapes += (pltpu.SMEM((slots + nears,), jnp.int32),)
                specs += (SMEM,)
            results = pl.pallas_call(
                lambda *refs, first=first: next_kernel(*refs, first=first),
                out_shape=shapes,
                in_specs=[SMEM] * (not first) + [VMEM] * 6 + [SMEM] * 3,
                out_specs=specs,
                scratch_shapes=[total, *staging],
                compiler_params=PARAMS,
                name="next_state",
            )(
                *(() if first else (ids,)), line_got, local, from_below, from_above,
                line_tiles, near_tiles, line_source, line_live, near_source,
            )
            state, terms, near_down, near_up = results[:4]
            ids = in_scalars(results[4])[0] if first else ids
            states.append(state)
        else:
            local, running = pl.pallas_call(
                last_local_kernel,
                out_shape=(sum_shape, pltpu.VMEM((blocks, rows, emb), f32)),
                in_specs=[VMEM, HBM, SMEM, VMEM, VMEM],
                out_specs=(VMEM, VMEM),
                scratch_shapes=local_scratch,
                compiler_params=PARAMS,
                name="last_local_sums",
            )(state, local_tiles, local_source, grad, states[1])
            out = pl.pallas_call(
                last_kernel,
                out_shape=jax.ShapeDtypeStruct((blocks, rows, emb), f32),
                in_specs=[SMEM] + [VMEM] * 5,
                out_specs=HBM,
                scratch_shapes=[total, pltpu.VMEM((blocks, rows, emb), f32), dma((blocks,))],
                compiler_params=PARAMS,
                name="last_state",
            )(ids, line_got, local, from_below, from_above, running)
    return out.reshape(blocks * rows, emb)


def solution(mesh):
    return jax.shard_map(
        on_device,
        mesh=mesh,
        in_specs=(
            P(("grp", "blk"), None),
            P(("grp", "blk"), None, None, None),
            P(("grp", "blk"), None),
            P("grp", "blk", None, None, None),
            P("grp", "blk", None),
            P("grp", "blk", None),
            P("grp", "blk", None, None, None),
            P("grp", "blk", None),
            P("grp", "blk", None),
            P("grp", "blk", None),
        ),
        out_specs=P(("grp", "blk"), None),
        check_vma=False,
    )
```

```python
import functools

import jax
import jax.numpy as jnp
from jax import lax
from jax.experimental import pallas as pl
from jax.experimental.pallas import tpu as pltpu
from jax.sharding import PartitionSpec as P

LAYERS = 3
ID_ROWS = 8
SENT_CHUNK = 2

VMEM = pl.BlockSpec(memory_space=pltpu.VMEM)
SMEM = pl.BlockSpec(memory_space=pltpu.SMEM)
HBM = pl.BlockSpec(memory_space=pltpu.HBM)
PARAMS = pltpu.CompilerParams(vmem_limit_bytes=8 * 2**20)


def on_chip(*arrays):
    return [pltpu.with_memory_space_constraint(array, pltpu.VMEM) for array in arrays]


def off_chip(*arrays):
    return [pltpu.with_memory_space_constraint(array, pltpu.HBM) for array in arrays]


def in_scalars(*arrays):
    return [pltpu.with_memory_space_constraint(array, pltpu.SMEM) for array in arrays]


def shifted(value, axis, steps):
    count = lax.axis_size(axis)
    leading, last = (max(0, -steps), min(count, count - steps))
    return lax.ppermute(value, axis, [(source, source + steps) for source in range(leading, last)])


def dot32(left, right):
    return jnp.dot(left, right, preferred_element_type=jnp.float32)


def id_rows(block_id, width):
    return jnp.full((ID_ROWS, width), block_id).astype(jnp.float32).astype(jnp.bfloat16)


def read_id(rows):
    return rows.astype(jnp.float32)[0, 0].astype(jnp.int32)


def send_copies(products, terms, sent):
    return [
        pltpu.make_async_copy(products.at[pl.ds(start, SENT_CHUNK)], terms.at[pl.ds(start, SENT_CHUNK)], sent.at[start // SENT_CHUNK])
        for start in range(0, terms.shape[0], SENT_CHUNK)
    ]


def line_products(state, tiles, source, live, terms, products, sent, target=None):
    slots, emb = terms.shape[0], state.shape[1]
    copies = send_copies(products, terms, sent)
    for slot in range(slots):
        product = dot32(state[source[0, 0, slot]], tiles[slot])
        products[slot, :emb] = (product * live[0, 0, slot].astype(jnp.float32)).astype(products.dtype)
        if target is not None:
            products[slot, emb:] = id_rows(target[0, 0, slot], products.shape[2])
        if slot % SENT_CHUNK == SENT_CHUNK - 1:
            copies[slot // SENT_CHUNK].start()


def wait_sent(products, terms, sent):
    for copy in send_copies(products, terms, sent):
        copy.wait()


def first_kernel(
    grad, line_tiles, line_from, line_live, line_to, near_from, near_to, source,
    state, terms, line_from_out, line_live_out, near_from_out, near_to_out, source_out,
    grad_in, line_in, line_to_in, products, sent, got, got_index,
):
    slots, blocks = terms.shape[0], state.shape[0]
    pairs = (
        (line_from, line_from_out), (line_live, line_live_out), (line_to, line_to_in),
        (near_from, near_from_out), (near_to, near_to_out), (source, source_out),
    )
    index_copies = [pltpu.make_async_copy(*pair, got_index.at[number]) for number, pair in enumerate(pairs)]
    half = blocks // 2
    grad_copies = [
        pltpu.make_async_copy(grad.at[pl.ds(start, half)], grad_in.at[pl.ds(start, half)], got.at[1 + start // half])
        for start in range(0, blocks, half)
    ]
    line_copy = pltpu.make_async_copy(line_tiles.at[0, 0], line_in, got.at[0])
    for copy in (*grad_copies, *index_copies, line_copy):
        copy.start()
    for block in range(blocks):
        if block % half == 0:
            grad_copies[block // half].wait()
        state[block] = grad_in[block].T
    for copy in (*index_copies[:3], line_copy):
        copy.wait()
    line_products(state, line_in, line_from_out, line_live_out, terms, products, sent, target=line_to_in)
    for copy in index_copies[3:]:
        copy.wait()
    wait_sent(products, terms, sent)


def local_kernel(state, tiles, near_tiles, source, near_from, near_to, *refs, last, with_ids):
    if last:
        grad, earlier, *refs = refs
    local, near_down, near_up, *refs = refs
    if last:
        running, *refs = refs
    tiles_in, near_in, got = refs
    blocks, per_block, rows, cols = tiles.shape
    emb = local.shape[1]
    near_copy = pltpu.make_async_copy(near_tiles.at[0, 0], near_in, got.at[blocks])
    copies = [pltpu.make_async_copy(tiles.at[block], tiles_in.at[block], got.at[block]) for block in range(blocks)]
    for copy in (near_copy, *copies):
        copy.start()
    if last:
        for block in range(blocks):
            running[block] = (
                grad[block].astype(jnp.float32)
                + earlier[block].T.astype(jnp.float32)
                + state[block].T.astype(jnp.float32)
            )
    near_copy.wait()
    for slot, near in enumerate((near_down, near_up)):
        near[:emb] = dot32(state[near_from[0, 0, slot]], near_in[slot]).astype(near.dtype)
        if with_ids:
            near[emb:] = id_rows(near_to[0, 0, slot], near.shape[1])
    for block in range(blocks):
        left = jnp.concatenate([state[source[block, k]] for k in range(per_block)], axis=1)
        copies[block].wait()
        local[block] = dot32(left, tiles_in[block].reshape(per_block * rows, cols))


def collect(ids, line_got, nears, total):
    slots, emb = line_got.shape[0], total.shape[1]
    for index, near in enumerate(nears):
        target = ids[slots + index]
        total[target] = total[target] + near[:emb].astype(jnp.float32)
    for slot in range(slots):
        target = ids[slot]
        total[target] = total[target] + line_got[slot, :emb].astype(jnp.float32)


def next_kernel(*refs, first):
    if first:
        line_got, local, from_below, from_above, *refs = refs
    else:
        ids, line_got, local, from_below, from_above, *refs = refs
    line_tiles, line_from, line_live, *refs = refs
    state, terms, total, *refs = refs
    if first:
        ids, *refs = refs
    products, sent = refs
    slots, emb = terms.shape[0], state.shape[1]
    if first:
        for slot in range(slots):
            ids[slot] = read_id(line_got[slot, emb:])
        for index, near in enumerate((from_below, from_above)):
            ids[slots + index] = read_id(near[emb:])
    collect(ids, line_got, (from_below, from_above), total)
    state[...] = total[...].astype(state.dtype)
    line_products(state, line_tiles.at[0, 0], line_from, line_live, terms, products, sent)
    wait_sent(products, terms, sent)


def last_kernel(ids, line_got, local, from_below, from_above, running, out, total, final, sent):
    collect(ids, line_got, (from_below, from_above), total)
    copies = [pltpu.make_async_copy(final.at[block], out.at[block], sent.at[block]) for block in range(out.shape[0])]
    for block, copy in enumerate(copies):
        newest = total[block].astype(jnp.bfloat16).T.astype(jnp.float32)
        final[block] = (running[block] + newest) * (1.0 / (LAYERS + 1))
        copy.start()
    for copy in copies:
        copy.wait()


def on_device(
    grad_final, local_tiles, local_source, near_tiles, near_source, near_target,
    line_tiles, line_source, line_target, line_live,
):
    blocks, per_block, rows, cols = local_tiles.shape
    emb = grad_final.shape[1]
    slots = line_tiles.shape[2]
    nears = near_tiles.shape[2]
    bf16, f32 = jnp.bfloat16, jnp.float32
    dma = pltpu.SemaphoreType.DMA
    grad = grad_final.reshape(blocks, rows, emb)
    state_shape = pltpu.VMEM((blocks, emb, rows), bf16)
    sum_shape = pltpu.VMEM((blocks, emb, rows), f32)

    def emitted(extra):
        terms = (slots, emb + extra, cols)
        return (state_shape, pltpu.HBM(terms, bf16)), (VMEM, HBM), [pltpu.VMEM(terms, bf16), dma((slots,))]

    shapes, specs, staging = emitted(ID_ROWS)
    indices = (line_source, line_live, near_source, near_target, local_source)
    state, terms, *indices = pl.pallas_call(
        first_kernel,
        out_shape=(*shapes, *(pltpu.SMEM(index.shape, jnp.int32) for index in indices)),
        in_specs=[HBM] * 8,
        out_specs=(*specs, *(SMEM for _ in indices)),
        scratch_shapes=[
            pltpu.VMEM((blocks, rows, emb), bf16),
            pltpu.VMEM((slots, rows, cols), bf16),
            pltpu.SMEM(line_target.shape, jnp.int32),
            *staging,
            dma((3,)),
            dma((6,)),
        ],
        compiler_params=PARAMS,
        name="first_terms",
    )(*off_chip(grad, line_tiles, line_source, line_live, line_target, near_source, near_target, local_source))
    line_source, line_live, near_source, near_target, local_source = in_scalars(*indices)
    local_tiles, near_tiles = off_chip(local_tiles, near_tiles)
    (line_tiles,) = on_chip(line_tiles)
    states, ids = [state], None
    for layer in range(LAYERS):
        first, last = layer == 0, layer == LAYERS - 1
        line_got = lax.all_to_all(terms, "blk", split_axis=0, concat_axis=0, tiled=True)
        near_shape = pltpu.VMEM((emb + ID_ROWS * first, cols), bf16)
        (state,) = on_chip(state)
        local, near_down, near_up, *running = pl.pallas_call(
            functools.partial(local_kernel, last=last, with_ids=first),
            out_shape=(sum_shape, near_shape, near_shape) + (pltpu.VMEM((blocks, rows, emb), f32),) * last,
            in_specs=[VMEM, HBM, HBM] + [SMEM] * 3 + [VMEM] * (2 * last),
            out_specs=(VMEM,) * (3 + last),
            scratch_shapes=[
                pltpu.VMEM(local_tiles.shape, bf16), pltpu.VMEM((nears, rows, cols), bf16), dma((blocks + 1,)),
            ],
            compiler_params=PARAMS,
            name="local_sums",
        )(
            state, local_tiles, near_tiles, local_source, near_source, near_target,
            *((grad, states[1]) if last else ()),
        )
        from_below = shifted(near_up, "grp", 1)
        from_above = shifted(near_down, "grp", -1)
        collected = on_chip(line_got, local, from_below, from_above)
        if not last:
            shapes, specs, staging = emitted(0)
            shapes += (sum_shape,) + (pltpu.SMEM((slots + nears,), jnp.int32),) * first
            specs += (VMEM,) + (SMEM,) * first
            state, terms, _, *new_ids = pl.pallas_call(
                functools.partial(next_kernel, first=first),
                out_shape=shapes,
                in_specs=[SMEM] * (not first) + [VMEM] * 5 + [SMEM] * 2,
                out_specs=specs,
                scratch_shapes=staging,
                input_output_aliases={2 - first: 2},
                compiler_params=PARAMS,
                name="next_state",
            )(*(() if first else (ids,)), *collected, line_tiles, line_source, line_live)
            if first:
                (ids,) = in_scalars(*new_ids)
            states.append(state)
        else:
            out, _ = pl.pallas_call(
                last_kernel,
                out_shape=(pltpu.HBM((blocks, rows, emb), f32), sum_shape),
                in_specs=[SMEM] + [VMEM] * 5,
                out_specs=(HBM, VMEM),
                input_output_aliases={2: 1},
                scratch_shapes=[pltpu.VMEM((blocks, rows, emb), f32), dma((blocks,))],
                compiler_params=PARAMS,
                name="last_state",
            )(ids, *collected, *running)
    return out.reshape(blocks * rows, emb)


def solution(mesh):
    return jax.shard_map(
        on_device,
        mesh=mesh,
        in_specs=(
            P(("grp", "blk"), None),
            P(("grp", "blk"), None, None, None),
            P(("grp", "blk"), None),
            P("grp", "blk", None, None, None),
            P("grp", "blk", None),
            P("grp", "blk", None),
            P("grp", "blk", None, None, None),
            P("grp", "blk", None),
            P("grp", "blk", None),
            P("grp", "blk", None),
        ),
        out_specs=P(("grp", "blk"), None),
        check_vma=False,
    )
```

```python
import functools

import jax
import jax.numpy as jnp
from jax import lax
from jax.experimental import pallas as pl
from jax.experimental.pallas import tpu as pltpu
from jax.sharding import PartitionSpec as P

LAYERS = 3
ID_ROWS = 8
SENT_CHUNK = 2

VMEM = pl.BlockSpec(memory_space=pltpu.VMEM)
SMEM = pl.BlockSpec(memory_space=pltpu.SMEM)
HBM = pl.BlockSpec(memory_space=pltpu.HBM)
PARAMS = pltpu.CompilerParams(vmem_limit_bytes=8 * 2**20)


def on_chip(*arrays):
    return [pltpu.with_memory_space_constraint(array, pltpu.VMEM) for array in arrays]


def off_chip(*arrays):
    return [pltpu.with_memory_space_constraint(array, pltpu.HBM) for array in arrays]


def in_scalars(*arrays):
    return [pltpu.with_memory_space_constraint(array, pltpu.SMEM) for array in arrays]


def shifted(value, axis, steps):
    count = lax.axis_size(axis)
    leading, last = (max(0, -steps), min(count, count - steps))
    return lax.ppermute(value, axis, [(source, source + steps) for source in range(leading, last)])


def dot32(left, right):
    return jnp.dot(left, right, preferred_element_type=jnp.float32)


def id_rows(block_id, width):
    return jnp.full((ID_ROWS, width), block_id).astype(jnp.float32).astype(jnp.bfloat16)


def read_id(rows):
    return rows.astype(jnp.float32)[0, 0].astype(jnp.int32)


def send_copies(products, terms, sent):
    return [
        pltpu.make_async_copy(products.at[pl.ds(start, SENT_CHUNK)], terms.at[pl.ds(start, SENT_CHUNK)], sent)
        for start in range(0, terms.shape[0], SENT_CHUNK)
    ]


def line_products(state, tiles, source, live, terms, products, sent, target=None):
    slots, emb = terms.shape[0], state.shape[1]
    copies = send_copies(products, terms, sent)
    for slot in range(slots):
        product = dot32(state[source[0, 0, slot]], tiles[slot])
        products[slot, :emb] = (product * live[0, 0, slot].astype(jnp.float32)).astype(products.dtype)
        if target is not None:
            products[slot, emb:] = id_rows(target[0, 0, slot], products.shape[2])
        if slot % SENT_CHUNK == SENT_CHUNK - 1:
            copies[slot // SENT_CHUNK].start()


def wait_sent(products, terms, sent):
    pltpu.make_async_copy(products, terms, sent).wait()


def first_kernel(
    grad, line_tiles, line_from, line_live, line_to, near_from, near_to, source,
    state, terms, line_from_out, line_live_out, near_from_out, near_to_out, source_out,
    grad_in, line_in, line_to_in, products, sent, got, got_index,
):
    slots, blocks = terms.shape[0], state.shape[0]
    pairs = (
        (line_from, line_from_out), (line_live, line_live_out), (line_to, line_to_in),
        (near_from, near_from_out), (near_to, near_to_out), (source, source_out),
    )
    index_copies = [pltpu.make_async_copy(*pair, got_index.at[number]) for number, pair in enumerate(pairs)]
    half = blocks // 2
    grad_copies = [
        pltpu.make_async_copy(grad.at[pl.ds(start, half)], grad_in.at[pl.ds(start, half)], got.at[1 + start // half])
        for start in range(0, blocks, half)
    ]
    line_copy = pltpu.make_async_copy(line_tiles.at[0, 0], line_in, got.at[0])
    for copy in (*grad_copies, *index_copies, line_copy):
        copy.start()
    for block in range(blocks):
        if block % half == 0:
            grad_copies[block // half].wait()
        state[block] = grad_in[block].T
    for copy in (*index_copies[:3], line_copy):
        copy.wait()
    line_products(state, line_in, line_from_out, line_live_out, terms, products, sent, target=line_to_in)
    for copy in index_copies[3:]:
        copy.wait()
    wait_sent(products, terms, sent)


def local_kernel(state, tiles, near_tiles, source, near_from, near_to, *refs, last, with_ids):
    if last:
        grad, earlier, *refs = refs
    local, near_down, near_up, *refs = refs
    if last:
        running, *refs = refs
    tiles_in, near_in, got = refs
    blocks, per_block, rows, cols = tiles.shape
    emb = local.shape[1]
    near_copy = pltpu.make_async_copy(near_tiles.at[0, 0], near_in, got.at[blocks])
    copies = [pltpu.make_async_copy(tiles.at[block], tiles_in.at[block], got.at[block]) for block in range(blocks)]
    for copy in (near_copy, *copies):
        copy.start()
    if last:
        for block in range(blocks):
            running[block] = (
                grad[block].astype(jnp.float32)
                + earlier[block].T.astype(jnp.float32)
                + state[block].T.astype(jnp.float32)
            )
    near_copy.wait()
    for slot, near in enumerate((near_down, near_up)):
        near[:emb] = dot32(state[near_from[0, 0, slot]], near_in[slot]).astype(near.dtype)
        if with_ids:
            near[emb:] = id_rows(near_to[0, 0, slot], near.shape[1])
    for block in range(blocks):
        left = jnp.concatenate([state[source[block, k]] for k in range(per_block)], axis=1)
        copies[block].wait()
        local[block] = dot32(left, tiles_in[block].reshape(per_block * rows, cols))


def collect(ids, line_got, nears, total):
    slots, emb = line_got.shape[0], total.shape[1]
    for index, near in enumerate(nears):
        target = ids[slots + index]
        total[target] = total[target] + near[:emb].astype(jnp.float32)
    for slot in range(slots):
        target = ids[slot]
        total[target] = total[target] + line_got[slot, :emb].astype(jnp.float32)


def next_kernel(*refs, first):
    if first:
        line_got, local, from_below, from_above, *refs = refs
    else:
        ids, line_got, local, from_below, from_above, *refs = refs
    line_tiles, line_from, line_live, *refs = refs
    state, terms, total, *refs = refs
    if first:
        ids, *refs = refs
    products, sent = refs
    slots, emb = terms.shape[0], state.shape[1]
    if first:
        for slot in range(slots):
            ids[slot] = read_id(line_got[slot, emb:])
        for index, near in enumerate((from_below, from_above)):
            ids[slots + index] = read_id(near[emb:])
    collect(ids, line_got, (from_below, from_above), total)
    state[...] = total[...].astype(state.dtype)
    line_products(state, line_tiles.at[0, 0], line_from, line_live, terms, products, sent)
    wait_sent(products, terms, sent)


def last_kernel(ids, line_got, local, from_below, from_above, running, out, total, final, sent):
    collect(ids, line_got, (from_below, from_above), total)
    copies = [pltpu.make_async_copy(final.at[block], out.at[block], sent) for block in range(out.shape[0])]
    for block, copy in enumerate(copies):
        newest = total[block].astype(jnp.bfloat16).T.astype(jnp.float32)
        final[block] = (running[block] + newest) * (1.0 / (LAYERS + 1))
        copy.start()
    wait_sent(final, out, sent)


def on_device(
    grad_final, local_tiles, local_source, near_tiles, near_source, near_target,
    line_tiles, line_source, line_target, line_live,
):
    blocks, per_block, rows, cols = local_tiles.shape
    emb = grad_final.shape[1]
    slots = line_tiles.shape[2]
    nears = near_tiles.shape[2]
    bf16, f32 = jnp.bfloat16, jnp.float32
    dma = pltpu.SemaphoreType.DMA
    grad = grad_final.reshape(blocks, rows, emb)
    state_shape = pltpu.VMEM((blocks, emb, rows), bf16)
    sum_shape = pltpu.VMEM((blocks, emb, rows), f32)

    def emitted(extra):
        terms = (slots, emb + extra, cols)
        return (state_shape, pltpu.HBM(terms, bf16)), (VMEM, HBM), [pltpu.VMEM(terms, bf16), dma]

    shapes, specs, staging = emitted(ID_ROWS)
    indices = (line_source, line_live, near_source, near_target, local_source)
    state, terms, *indices = pl.pallas_call(
        first_kernel,
        out_shape=(*shapes, *(pltpu.SMEM(index.shape, jnp.int32) for index in indices)),
        in_specs=[HBM] * 8,
        out_specs=(*specs, *(SMEM for _ in indices)),
        scratch_shapes=[
            pltpu.VMEM((blocks, rows, emb), bf16),
            pltpu.VMEM((slots, rows, cols), bf16),
            pltpu.SMEM(line_target.shape, jnp.int32),
            *staging,
            dma((3,)),
            dma((6,)),
        ],
        compiler_params=PARAMS,
        name="first_terms",
    )(*off_chip(grad, line_tiles, line_source, line_live, line_target, near_source, near_target, local_source))
    line_source, line_live, near_source, near_target, local_source = in_scalars(*indices)
    local_tiles, near_tiles = off_chip(local_tiles, near_tiles)
    (line_tiles,) = on_chip(line_tiles)
    states, ids = [state], None
    for layer in range(LAYERS):
        first, last = layer == 0, layer == LAYERS - 1
        line_got = lax.all_to_all(terms, "blk", split_axis=0, concat_axis=0, tiled=True)
        near_shape = pltpu.VMEM((emb + ID_ROWS * first, cols), bf16)
        (state,) = on_chip(state)
        local, near_down, near_up, *running = pl.pallas_call(
            functools.partial(local_kernel, last=last, with_ids=first),
            out_shape=(sum_shape, near_shape, near_shape) + (pltpu.VMEM((blocks, rows, emb), f32),) * last,
            in_specs=[VMEM, HBM, HBM] + [SMEM] * 3 + [VMEM] * (2 * last),
            out_specs=(VMEM,) * (3 + last),
            scratch_shapes=[
                pltpu.VMEM(local_tiles.shape, bf16), pltpu.VMEM((nears, rows, cols), bf16), dma((blocks + 1,)),
            ],
            compiler_params=PARAMS,
            name="local_sums",
        )(
            state, local_tiles, near_tiles, local_source, near_source, near_target,
            *((grad, states[1]) if last else ()),
        )
        from_below = shifted(near_up, "grp", 1)
        from_above = shifted(near_down, "grp", -1)
        collected = on_chip(line_got, local, from_below, from_above)
        if not last:
            shapes, specs, staging = emitted(0)
            shapes += (sum_shape,) + (pltpu.SMEM((slots + nears,), jnp.int32),) * first
            specs += (VMEM,) + (SMEM,) * first
            state, terms, _, *new_ids = pl.pallas_call(
                functools.partial(next_kernel, first=first),
                out_shape=shapes,
                in_specs=[SMEM] * (not first) + [VMEM] * 5 + [SMEM] * 2,
                out_specs=specs,
                scratch_shapes=staging,
                input_output_aliases={2 - first: 2},
                compiler_params=PARAMS,
                name="next_state",
            )(*(() if first else (ids,)), *collected, line_tiles, line_source, line_live)
            if first:
                (ids,) = in_scalars(*new_ids)
            states.append(state)
        else:
            out, _ = pl.pallas_call(
                last_kernel,
                out_shape=(pltpu.HBM((blocks, rows, emb), f32), sum_shape),
                in_specs=[SMEM] + [VMEM] * 5,
                out_specs=(HBM, VMEM),
                input_output_aliases={2: 1},
                scratch_shapes=[pltpu.VMEM((blocks, rows, emb), f32), dma],
                compiler_params=PARAMS,
                name="last_state",
            )(ids, *collected, *running)
    return out.reshape(blocks * rows, emb)


def solution(mesh):
    return jax.shard_map(
        on_device,
        mesh=mesh,
        in_specs=(
            P(("grp", "blk"), None),
            P(("grp", "blk"), None, None, None),
            P(("grp", "blk"), None),
            P("grp", "blk", None, None, None),
            P("grp", "blk", None),
            P("grp", "blk", None),
            P("grp", "blk", None, None, None),
            P("grp", "blk", None),
            P("grp", "blk", None),
            P("grp", "blk", None),
        ),
        out_specs=P(("grp", "blk"), None),
        check_vma=False,
    )
```

```python
import functools

import jax
import jax.numpy as jnp
from jax import lax
from jax.experimental import pallas as pl
from jax.experimental.pallas import tpu as pltpu
from jax.sharding import PartitionSpec as P

LAYERS = 3
ID_ROWS = 8
SENT_CHUNK = 2

VMEM = pl.BlockSpec(memory_space=pltpu.VMEM)
SMEM = pl.BlockSpec(memory_space=pltpu.SMEM)
HBM = pl.BlockSpec(memory_space=pltpu.HBM)
PARAMS = pltpu.CompilerParams(vmem_limit_bytes=8 * 2**20)


def on_chip(*arrays):
    return [pltpu.with_memory_space_constraint(array, pltpu.VMEM) for array in arrays]


def off_chip(*arrays):
    return [pltpu.with_memory_space_constraint(array, pltpu.HBM) for array in arrays]


def in_scalars(*arrays):
    return [pltpu.with_memory_space_constraint(array, pltpu.SMEM) for array in arrays]


def shifted(value, axis, steps):
    count = lax.axis_size(axis)
    leading, last = (max(0, -steps), min(count, count - steps))
    return lax.ppermute(value, axis, [(source, source + steps) for source in range(leading, last)])


def dot32(left, right):
    return jnp.dot(left, right, preferred_element_type=jnp.float32)


def id_rows(block_id, width):
    return jnp.full((ID_ROWS, width), block_id).astype(jnp.float32).astype(jnp.bfloat16)


def read_id(rows):
    return rows.astype(jnp.float32)[0, 0].astype(jnp.int32)


def send_copies(products, terms, sent):
    return [
        pltpu.make_async_copy(products.at[pl.ds(start, SENT_CHUNK)], terms.at[pl.ds(start, SENT_CHUNK)], sent)
        for start in range(0, terms.shape[0], SENT_CHUNK)
    ]


def line_products(state, tiles, source, live, terms, products, sent, target=None):
    slots, emb = terms.shape[0], state.shape[1]
    copies = send_copies(products, terms, sent)
    for slot in range(slots):
        product = dot32(state[source[0, 0, slot]], tiles[slot])
        products[slot, :emb] = (product * live[0, 0, slot].astype(jnp.float32)).astype(products.dtype)
        if target is not None:
            products[slot, emb:] = id_rows(target[0, 0, slot], products.shape[2])
        if slot % SENT_CHUNK == SENT_CHUNK - 1:
            copies[slot // SENT_CHUNK].start()


def wait_sent(products, terms, sent):
    pltpu.make_async_copy(products, terms, sent).wait()


def first_kernel(
    grad, line_tiles, line_from, line_live, line_to, near_from, near_to, source,
    state, terms, line_from_out, line_live_out, near_from_out, near_to_out, source_out,
    grad_in, line_in, line_to_in, products, sent, got, got_index,
):
    slots, blocks = terms.shape[0], state.shape[0]
    pairs = (
        (line_from, line_from_out), (line_live, line_live_out), (line_to, line_to_in),
        (near_from, near_from_out), (near_to, near_to_out), (source, source_out),
    )
    index_copies = [pltpu.make_async_copy(*pair, got_index.at[number]) for number, pair in enumerate(pairs)]
    half = blocks // 2
    grad_copies = [
        pltpu.make_async_copy(grad.at[pl.ds(start, half)], grad_in.at[pl.ds(start, half)], got.at[1 + start // half])
        for start in range(0, blocks, half)
    ]
    line_copy = pltpu.make_async_copy(line_tiles.at[0, 0], line_in, got.at[0])
    for copy in (*grad_copies, *index_copies, line_copy):
        copy.start()
    for block in range(blocks):
        if block % half == 0:
            grad_copies[block // half].wait()
        state[block] = grad_in[block].T
    for copy in (*index_copies[:3], line_copy):
        copy.wait()
    line_products(state, line_in, line_from_out, line_live_out, terms, products, sent, target=line_to_in)
    for copy in index_copies[3:]:
        copy.wait()
    wait_sent(products, terms, sent)


def near_kernel(state, tiles, source, target, near_down, near_up, *, with_ids):
    emb = state.shape[1]
    for slot, near in enumerate((near_down, near_up)):
        near[:emb] = dot32(state[source[0, 0, slot]], tiles[0, 0, slot]).astype(near.dtype)
        if with_ids:
            near[emb:] = id_rows(target[0, 0, slot], near.shape[1])


def local_kernel(state, tiles, source, *refs, last):
    if last:
        grad, earlier, *refs = refs
    local, *refs = refs
    if last:
        running, *refs = refs
    tiles_in, got = refs
    blocks, per_block, rows, cols = tiles.shape
    copies = [pltpu.make_async_copy(tiles.at[block], tiles_in.at[block], got.at[block]) for block in range(blocks)]
    for copy in copies:
        copy.start()
    if last:
        for block in range(blocks):
            running[block] = (
                grad[block].astype(jnp.float32)
                + earlier[block].T.astype(jnp.float32)
                + state[block].T.astype(jnp.float32)
            )
    for block in range(blocks):
        left = jnp.concatenate([state[source[block, k]] for k in range(per_block)], axis=1)
        copies[block].wait()
        local[block] = dot32(left, tiles_in[block].reshape(per_block * rows, cols))


def collect(ids, line_got, nears, total):
    slots, emb = line_got.shape[0], total.shape[1]
    for index, near in enumerate(nears):
        target = ids[slots + index]
        total[target] = total[target] + near[:emb].astype(jnp.float32)
    for slot in range(slots):
        target = ids[slot]
        total[target] = total[target] + line_got[slot, :emb].astype(jnp.float32)


def next_kernel(*refs, first):
    if first:
        line_got, local, from_below, from_above, *refs = refs
    else:
        ids, line_got, local, from_below, from_above, *refs = refs
    line_tiles, line_from, line_live, *refs = refs
    state, terms, total, *refs = refs
    if first:
        ids, *refs = refs
    products, sent = refs
    slots, emb = terms.shape[0], state.shape[1]
    if first:
        for slot in range(slots):
            ids[slot] = read_id(line_got[slot, emb:])
        for index, near in enumerate((from_below, from_above)):
            ids[slots + index] = read_id(near[emb:])
    collect(ids, line_got, (from_below, from_above), total)
    state[...] = total[...].astype(state.dtype)
    line_products(state, line_tiles.at[0, 0], line_from, line_live, terms, products, sent)
    wait_sent(products, terms, sent)


def last_kernel(ids, line_got, local, from_below, from_above, running, out, total, final, sent):
    collect(ids, line_got, (from_below, from_above), total)
    copies = [pltpu.make_async_copy(final.at[block], out.at[block], sent) for block in range(out.shape[0])]
    for block, copy in enumerate(copies):
        newest = total[block].astype(jnp.bfloat16).T.astype(jnp.float32)
        final[block] = (running[block] + newest) * (1.0 / (LAYERS + 1))
        copy.start()
    wait_sent(final, out, sent)


def on_device(
    grad_final, local_tiles, local_source, near_tiles, near_source, near_target,
    line_tiles, line_source, line_target, line_live,
):
    blocks, per_block, rows, cols = local_tiles.shape
    emb = grad_final.shape[1]
    slots = line_tiles.shape[2]
    nears = near_tiles.shape[2]
    bf16, f32 = jnp.bfloat16, jnp.float32
    dma = pltpu.SemaphoreType.DMA
    grad = grad_final.reshape(blocks, rows, emb)
    state_shape = pltpu.VMEM((blocks, emb, rows), bf16)
    sum_shape = pltpu.VMEM((blocks, emb, rows), f32)

    def emitted(extra):
        terms = (slots, emb + extra, cols)
        return (state_shape, pltpu.HBM(terms, bf16)), (VMEM, HBM), [pltpu.VMEM(terms, bf16), dma]

    shapes, specs, staging = emitted(ID_ROWS)
    indices = (line_source, line_live, near_source, near_target, local_source)
    state, terms, *indices = pl.pallas_call(
        first_kernel,
        out_shape=(*shapes, *(pltpu.SMEM(index.shape, jnp.int32) for index in indices)),
        in_specs=[HBM] * 8,
        out_specs=(*specs, *(SMEM for _ in indices)),
        scratch_shapes=[
            pltpu.VMEM((blocks, rows, emb), bf16),
            pltpu.VMEM((slots, rows, cols), bf16),
            pltpu.SMEM(line_target.shape, jnp.int32),
            *staging,
            dma((3,)),
            dma((6,)),
        ],
        compiler_params=PARAMS,
        name="first_terms",
    )(*off_chip(grad, line_tiles, line_source, line_live, line_target, near_source, near_target, local_source))
    line_source, line_live, near_source, near_target, local_source = in_scalars(*indices)
    (local_tiles,) = off_chip(local_tiles)
    line_tiles, near_tiles = on_chip(line_tiles, near_tiles)
    states, ids = [state], None
    for layer in range(LAYERS):
        first, last = layer == 0, layer == LAYERS - 1
        line_got = lax.all_to_all(terms, "blk", split_axis=0, concat_axis=0, tiled=True)
        near_shape = pltpu.VMEM((emb + ID_ROWS * first, cols), bf16)
        (state,) = on_chip(state)
        near_down, near_up = pl.pallas_call(
            functools.partial(near_kernel, with_ids=first),
            out_shape=(near_shape, near_shape),
            in_specs=[VMEM] * 2 + [SMEM] * 2,
            out_specs=(VMEM, VMEM),
            compiler_params=PARAMS,
            name="near_terms",
        )(state, near_tiles, near_source, near_target)
        local, *running = pl.pallas_call(
            functools.partial(local_kernel, last=last),
            out_shape=(sum_shape,) + (pltpu.VMEM((blocks, rows, emb), f32),) * last,
            in_specs=[VMEM, HBM, SMEM] + [VMEM] * (2 * last),
            out_specs=(VMEM,) * (1 + last),
            scratch_shapes=[
                pltpu.VMEM(local_tiles.shape, bf16), dma((blocks,)),
            ],
            compiler_params=PARAMS,
            name="local_sums",
        )(
            state, local_tiles, local_source,
            *((grad, states[1]) if last else ()),
        )
        from_below = shifted(near_up, "grp", 1)
        from_above = shifted(near_down, "grp", -1)
        collected = on_chip(line_got, local, from_below, from_above)
        if not last:
            shapes, specs, staging = emitted(0)
            shapes += (sum_shape,) + (pltpu.SMEM((slots + nears,), jnp.int32),) * first
            specs += (VMEM,) + (SMEM,) * first
            state, terms, _, *new_ids = pl.pallas_call(
                functools.partial(next_kernel, first=first),
                out_shape=shapes,
                in_specs=[SMEM] * (not first) + [VMEM] * 5 + [SMEM] * 2,
                out_specs=specs,
                scratch_shapes=staging,
                input_output_aliases={2 - first: 2},
                compiler_params=PARAMS,
                name="next_state",
            )(*(() if first else (ids,)), *collected, line_tiles, line_source, line_live)
            if first:
                (ids,) = in_scalars(*new_ids)
            states.append(state)
        else:
            out, _ = pl.pallas_call(
                last_kernel,
                out_shape=(pltpu.HBM((blocks, rows, emb), f32), sum_shape),
                in_specs=[SMEM] + [VMEM] * 5,
                out_specs=(HBM, VMEM),
                input_output_aliases={2: 1},
                scratch_shapes=[pltpu.VMEM((blocks, rows, emb), f32), dma],
                compiler_params=PARAMS,
                name="last_state",
            )(ids, *collected, *running)
    return out.reshape(blocks * rows, emb)


def solution(mesh):
    return jax.shard_map(
        on_device,
        mesh=mesh,
        in_specs=(
            P(("grp", "blk"), None),
            P(("grp", "blk"), None, None, None),
            P(("grp", "blk"), None),
            P("grp", "blk", None, None, None),
            P("grp", "blk", None),
            P("grp", "blk", None),
            P("grp", "blk", None, None, None),
            P("grp", "blk", None),
            P("grp", "blk", None),
            P("grp", "blk", None),
        ),
        out_specs=P(("grp", "blk"), None),
        check_vma=False,
    )
```

```python
import functools

import jax
import jax.numpy as jnp
from jax import lax
from jax.experimental import pallas as pl
from jax.experimental.pallas import tpu as pltpu
from jax.sharding import PartitionSpec as P

LAYERS = 3
ID_ROWS = 8
SENT_CHUNK = 2

VMEM = pl.BlockSpec(memory_space=pltpu.VMEM)
SMEM = pl.BlockSpec(memory_space=pltpu.SMEM)
HBM = pl.BlockSpec(memory_space=pltpu.HBM)
PARAMS = pltpu.CompilerParams(vmem_limit_bytes=8 * 2**20)


def on_chip(*arrays):
    return [pltpu.with_memory_space_constraint(array, pltpu.VMEM) for array in arrays]


def off_chip(*arrays):
    return [pltpu.with_memory_space_constraint(array, pltpu.HBM) for array in arrays]


def in_scalars(*arrays):
    return [pltpu.with_memory_space_constraint(array, pltpu.SMEM) for array in arrays]


def shifted(value, axis, steps):
    count = lax.axis_size(axis)
    leading, last = (max(0, -steps), min(count, count - steps))
    return lax.ppermute(value, axis, [(source, source + steps) for source in range(leading, last)])


def dot32(left, right):
    return jnp.dot(left, right, preferred_element_type=jnp.float32)


def id_rows(block_id, width):
    return jnp.full((ID_ROWS, width), block_id).astype(jnp.float32).astype(jnp.bfloat16)


def read_id(rows):
    return rows.astype(jnp.float32)[0, 0].astype(jnp.int32)


def send_copies(products, terms, sent):
    return [
        pltpu.make_async_copy(products.at[pl.ds(start, SENT_CHUNK)], terms.at[pl.ds(start, SENT_CHUNK)], sent)
        for start in range(0, terms.shape[0], SENT_CHUNK)
    ]


def line_products(state, tiles, source, live, terms, products, sent, target=None):
    slots, emb = terms.shape[0], state.shape[1]
    copies = send_copies(products, terms, sent)
    for slot in range(slots):
        product = dot32(state[source[0, 0, slot]], tiles[slot])
        products[slot, :emb] = (product * live[0, 0, slot].astype(jnp.float32)).astype(products.dtype)
        if target is not None:
            products[slot, emb:] = id_rows(target[0, 0, slot], products.shape[2])
        if slot % SENT_CHUNK == SENT_CHUNK - 1:
            copies[slot // SENT_CHUNK].start()


def wait_sent(products, terms, sent):
    pltpu.make_async_copy(products, terms, sent).wait()


def first_kernel(
    grad, line_tiles, line_from, line_live, line_to, near_from, near_to, source,
    state, terms, line_from_out, line_live_out, near_from_out, near_to_out, source_out,
    grad_in, line_in, line_to_in, products, sent, got, got_index,
):
    slots, blocks = terms.shape[0], state.shape[0]
    pairs = (
        (line_from, line_from_out), (line_live, line_live_out), (line_to, line_to_in),
        (near_from, near_from_out), (near_to, near_to_out), (source, source_out),
    )
    index_copies = [pltpu.make_async_copy(*pair, got_index.at[number]) for number, pair in enumerate(pairs)]
    half = blocks // 2
    grad_copies = [
        pltpu.make_async_copy(grad.at[pl.ds(start, half)], grad_in.at[pl.ds(start, half)], got.at[1 + start // half])
        for start in range(0, blocks, half)
    ]
    line_copy = pltpu.make_async_copy(line_tiles.at[0, 0], line_in, got.at[0])
    for copy in (*grad_copies, *index_copies, line_copy):
        copy.start()
    for block in range(blocks):
        if block % half == 0:
            grad_copies[block // half].wait()
        state[block] = grad_in[block].T
    for copy in (*index_copies[:3], line_copy):
        copy.wait()
    line_products(state, line_in, line_from_out, line_live_out, terms, products, sent, target=line_to_in)
    for copy in index_copies[3:]:
        copy.wait()
    wait_sent(products, terms, sent)


def near_kernel(state, tiles, source, target, near_down, near_up, *, with_ids):
    emb = state.shape[1]
    for slot, near in enumerate((near_down, near_up)):
        near[:emb] = dot32(state[source[0, 0, slot]], tiles[0, 0, slot]).astype(near.dtype)
        if with_ids:
            near[emb:] = id_rows(target[0, 0, slot], near.shape[1])


def local_kernel(state, tiles, source, *refs, last):
    if last:
        grad, earlier, *refs = refs
    local, zeros, *refs = refs
    zeros[...] = jnp.zeros_like(zeros)
    if last:
        running, *refs = refs
    tiles_in, got = refs
    blocks, per_block, rows, cols = tiles.shape
    copies = [pltpu.make_async_copy(tiles.at[block], tiles_in.at[block], got.at[block]) for block in range(blocks)]
    for copy in copies:
        copy.start()
    if last:
        for block in range(blocks):
            running[block] = (
                grad[block].astype(jnp.float32)
                + earlier[block].T.astype(jnp.float32)
                + state[block].T.astype(jnp.float32)
            )
    for block in range(blocks):
        left = jnp.concatenate([state[source[block, k]] for k in range(per_block)], axis=1)
        copies[block].wait()
        local[block] = dot32(left, tiles_in[block].reshape(per_block * rows, cols))


def collect(ids, line_got, nears, sums):
    slots, emb = line_got.shape[0], sums[0].shape[1]
    for index in range(slots + len(nears)):
        term = line_got[index, :emb] if index < slots else nears[index - slots][:emb]
        total, target = sums[index % len(sums)], ids[index]
        total[target] = total[target] + term.astype(jnp.float32)


def next_kernel(*refs, first):
    if first:
        line_got, _, _, from_below, from_above, *refs = refs
    else:
        ids, line_got, _, _, from_below, from_above, *refs = refs
    line_tiles, line_from, line_live, *refs = refs
    state, terms, total, extra, *refs = refs
    if first:
        ids, *refs = refs
    products, sent = refs
    slots, emb = terms.shape[0], state.shape[1]
    if first:
        for slot in range(slots):
            ids[slot] = read_id(line_got[slot, emb:])
        for index, near in enumerate((from_below, from_above)):
            ids[slots + index] = read_id(near[emb:])
    collect(ids, line_got, (from_below, from_above), (total, extra))
    state[...] = (total[...] + extra[...]).astype(state.dtype)
    line_products(state, line_tiles.at[0, 0], line_from, line_live, terms, products, sent)
    wait_sent(products, terms, sent)


def last_kernel(ids, line_got, local, zeros, from_below, from_above, running, out, total, extra, final, sent):
    collect(ids, line_got, (from_below, from_above), (total, extra))
    copies = [pltpu.make_async_copy(final.at[block], out.at[block], sent) for block in range(out.shape[0])]
    for block, copy in enumerate(copies):
        newest = (total[block] + extra[block]).astype(jnp.bfloat16).T.astype(jnp.float32)
        final[block] = (running[block] + newest) * (1.0 / (LAYERS + 1))
        copy.start()
    wait_sent(final, out, sent)


def on_device(
    grad_final, local_tiles, local_source, near_tiles, near_source, near_target,
    line_tiles, line_source, line_target, line_live,
):
    blocks, per_block, rows, cols = local_tiles.shape
    emb = grad_final.shape[1]
    slots = line_tiles.shape[2]
    nears = near_tiles.shape[2]
    bf16, f32 = jnp.bfloat16, jnp.float32
    dma = pltpu.SemaphoreType.DMA
    grad = grad_final.reshape(blocks, rows, emb)
    state_shape = pltpu.VMEM((blocks, emb, rows), bf16)
    sum_shape = pltpu.VMEM((blocks, emb, rows), f32)

    def emitted(extra):
        terms = (slots, emb + extra, cols)
        return (state_shape, pltpu.HBM(terms, bf16)), (VMEM, HBM), [pltpu.VMEM(terms, bf16), dma]

    shapes, specs, staging = emitted(ID_ROWS)
    indices = (line_source, line_live, near_source, near_target, local_source)
    state, terms, *indices = pl.pallas_call(
        first_kernel,
        out_shape=(*shapes, *(pltpu.SMEM(index.shape, jnp.int32) for index in indices)),
        in_specs=[HBM] * 8,
        out_specs=(*specs, *(SMEM for _ in indices)),
        scratch_shapes=[
            pltpu.VMEM((blocks, rows, emb), bf16),
            pltpu.VMEM((slots, rows, cols), bf16),
            pltpu.SMEM(line_target.shape, jnp.int32),
            *staging,
            dma((3,)),
            dma((6,)),
        ],
        compiler_params=PARAMS,
        name="first_terms",
    )(*off_chip(grad, line_tiles, line_source, line_live, line_target, near_source, near_target, local_source))
    line_source, line_live, near_source, near_target, local_source = in_scalars(*indices)
    (local_tiles,) = off_chip(local_tiles)
    line_tiles, near_tiles = on_chip(line_tiles, near_tiles)
    states, ids = [state], None
    for layer in range(LAYERS):
        first, last = layer == 0, layer == LAYERS - 1
        line_got = lax.all_to_all(terms, "blk", split_axis=0, concat_axis=0, tiled=True)
        near_shape = pltpu.VMEM((emb + ID_ROWS * first, cols), bf16)
        (state,) = on_chip(state)
        near_down, near_up = pl.pallas_call(
            functools.partial(near_kernel, with_ids=first),
            out_shape=(near_shape, near_shape),
            in_specs=[VMEM] * 2 + [SMEM] * 2,
            out_specs=(VMEM, VMEM),
            compiler_params=PARAMS,
            name="near_terms",
        )(state, near_tiles, near_source, near_target)
        local, zeros, *running = pl.pallas_call(
            functools.partial(local_kernel, last=last),
            out_shape=(sum_shape, sum_shape) + (pltpu.VMEM((blocks, rows, emb), f32),) * last,
            in_specs=[VMEM, HBM, SMEM] + [VMEM] * (2 * last),
            out_specs=(VMEM,) * (2 + last),
            scratch_shapes=[
                pltpu.VMEM(local_tiles.shape, bf16), dma((blocks,)),
            ],
            compiler_params=PARAMS,
            name="local_sums",
        )(
            state, local_tiles, local_source,
            *((grad, states[1]) if last else ()),
        )
        from_below = shifted(near_up, "grp", 1)
        from_above = shifted(near_down, "grp", -1)
        collected = on_chip(line_got, local, zeros, from_below, from_above)
        if not last:
            shapes, specs, staging = emitted(0)
            shapes += (sum_shape, sum_shape) + (pltpu.SMEM((slots + nears,), jnp.int32),) * first
            specs += (VMEM, VMEM) + (SMEM,) * first
            state, terms, _, _, *new_ids = pl.pallas_call(
                functools.partial(next_kernel, first=first),
                out_shape=shapes,
                in_specs=[SMEM] * (not first) + [VMEM] * 6 + [SMEM] * 2,
                out_specs=specs,
                scratch_shapes=staging,
                input_output_aliases={2 - first: 2, 3 - first: 3},
                compiler_params=PARAMS,
                name="next_state",
            )(*(() if first else (ids,)), *collected, line_tiles, line_source, line_live)
            if first:
                (ids,) = in_scalars(*new_ids)
            states.append(state)
        else:
            out, _, _ = pl.pallas_call(
                last_kernel,
                out_shape=(pltpu.HBM((blocks, rows, emb), f32), sum_shape, sum_shape),
                in_specs=[SMEM] + [VMEM] * 6,
                out_specs=(HBM, VMEM, VMEM),
                input_output_aliases={2: 1, 3: 2},
                scratch_shapes=[pltpu.VMEM((blocks, rows, emb), f32), dma],
                compiler_params=PARAMS,
                name="last_state",
            )(ids, *collected, *running)
    return out.reshape(blocks * rows, emb)


def solution(mesh):
    return jax.shard_map(
        on_device,
        mesh=mesh,
        in_specs=(
            P(("grp", "blk"), None),
            P(("grp", "blk"), None, None, None),
            P(("grp", "blk"), None),
            P("grp", "blk", None, None, None),
            P("grp", "blk", None),
            P("grp", "blk", None),
            P("grp", "blk", None, None, None),
            P("grp", "blk", None),
            P("grp", "blk", None),
            P("grp", "blk", None),
        ),
        out_specs=P(("grp", "blk"), None),
        check_vma=False,
    )
```

```python
import functools

import jax
import jax.numpy as jnp
from jax import lax
from jax.experimental import pallas as pl
from jax.experimental.pallas import tpu as pltpu
from jax.sharding import PartitionSpec as P

LAYERS = 3
ID_ROWS = 8
SENT_CHUNK = 2

VMEM = pl.BlockSpec(memory_space=pltpu.VMEM)
SMEM = pl.BlockSpec(memory_space=pltpu.SMEM)
HBM = pl.BlockSpec(memory_space=pltpu.HBM)
PARAMS = pltpu.CompilerParams(vmem_limit_bytes=8 * 2**20)


def on_chip(*arrays):
    return [pltpu.with_memory_space_constraint(array, pltpu.VMEM) for array in arrays]


def off_chip(*arrays):
    return [pltpu.with_memory_space_constraint(array, pltpu.HBM) for array in arrays]


def in_scalars(*arrays):
    return [pltpu.with_memory_space_constraint(array, pltpu.SMEM) for array in arrays]


def shifted(value, axis, steps):
    count = lax.axis_size(axis)
    leading, last = (max(0, -steps), min(count, count - steps))
    return lax.ppermute(value, axis, [(source, source + steps) for source in range(leading, last)])


def dot32(left, right):
    return jnp.dot(left, right, preferred_element_type=jnp.float32)


def id_rows(block_id, width):
    return jnp.full((ID_ROWS, width), block_id).astype(jnp.float32).astype(jnp.bfloat16)


def read_id(rows):
    return rows.astype(jnp.float32)[0, 0].astype(jnp.int32)


def send_copies(products, terms, sent):
    return [
        pltpu.make_async_copy(products.at[pl.ds(start, SENT_CHUNK)], terms.at[pl.ds(start, SENT_CHUNK)], sent)
        for start in range(0, terms.shape[0], SENT_CHUNK)
    ]


def line_products(state, tiles, source, live, terms, products, sent, target=None):
    slots, emb = terms.shape[0], state.shape[1]
    copies = send_copies(products, terms, sent)
    for slot in range(slots):
        product = dot32(state[source[0, 0, slot]], tiles[slot])
        products[slot, :emb] = (product * live[0, 0, slot].astype(jnp.float32)).astype(products.dtype)
        if target is not None:
            products[slot, emb:] = id_rows(target[0, 0, slot], products.shape[2])
        if slot % SENT_CHUNK == SENT_CHUNK - 1:
            copies[slot // SENT_CHUNK].start()


def wait_sent(products, terms, sent):
    pltpu.make_async_copy(products, terms, sent).wait()


def first_kernel(
    grad, line_tiles, line_from, line_live, line_to, near_from, near_to, source,
    state, terms, line_from_out, line_live_out, near_from_out, near_to_out, source_out,
    grad_in, line_in, line_to_in, products, sent, got, got_index,
):
    slots, blocks = terms.shape[0], state.shape[0]
    pairs = (
        (line_from, line_from_out), (line_live, line_live_out), (line_to, line_to_in),
        (near_from, near_from_out), (near_to, near_to_out), (source, source_out),
    )
    index_copies = [pltpu.make_async_copy(*pair, got_index.at[number]) for number, pair in enumerate(pairs)]
    grad_copy = pltpu.make_async_copy(grad, grad_in, got.at[1])
    line_copy = pltpu.make_async_copy(line_tiles.at[0, 0], line_in, got.at[0])
    for copy in (grad_copy, *index_copies, line_copy):
        copy.start()
    grad_copy.wait()
    for block in range(blocks):
        state[block] = grad_in[block].T
    for copy in (*index_copies[:3], line_copy):
        copy.wait()
    line_products(state, line_in, line_from_out, line_live_out, terms, products, sent, target=line_to_in)
    for copy in index_copies[3:]:
        copy.wait()
    wait_sent(products, terms, sent)


def near_kernel(state, tiles, source, target, near_down, near_up, *, with_ids):
    emb = state.shape[1]
    for slot, near in enumerate((near_down, near_up)):
        near[:emb] = dot32(state[source[0, 0, slot]], tiles[0, 0, slot]).astype(near.dtype)
        if with_ids:
            near[emb:] = id_rows(target[0, 0, slot], near.shape[1])


def local_kernel(state, tiles, source, *refs, last):
    if last:
        grad, earlier, *refs = refs
    local, zeros, *refs = refs
    zeros[...] = jnp.zeros_like(zeros)
    if last:
        running, *refs = refs
    tiles_in, got = refs
    blocks, per_block, rows, cols = tiles.shape
    copies = [pltpu.make_async_copy(tiles.at[block], tiles_in.at[block], got.at[block]) for block in range(blocks)]
    for copy in copies:
        copy.start()
    if last:
        for block in range(blocks):
            running[block] = (
                grad[block].astype(jnp.float32)
                + earlier[block].T.astype(jnp.float32)
                + state[block].T.astype(jnp.float32)
            )
    for block in range(blocks):
        left = jnp.concatenate([state[source[block, k]] for k in range(per_block)], axis=1)
        copies[block].wait()
        local[block] = dot32(left, tiles_in[block].reshape(per_block * rows, cols))


def collect(ids, line_got, nears, sums):
    slots, emb = line_got.shape[0], sums[0].shape[1]
    for index in range(slots + len(nears)):
        term = line_got[index, :emb] if index < slots else nears[index - slots][:emb]
        total, target = sums[index % len(sums)], ids[index]
        total[target] = total[target] + term.astype(jnp.float32)


def next_kernel(*refs, first):
    if first:
        line_got, _, _, from_below, from_above, *refs = refs
    else:
        ids, line_got, _, _, from_below, from_above, *refs = refs
    line_tiles, line_from, line_live, *refs = refs
    state, terms, total, extra, *refs = refs
    if first:
        ids, *refs = refs
    products, sent = refs
    slots, emb = terms.shape[0], state.shape[1]
    if first:
        for slot in range(slots):
            ids[slot] = read_id(line_got[slot, emb:])
        for index, near in enumerate((from_below, from_above)):
            ids[slots + index] = read_id(near[emb:])
    collect(ids, line_got, (from_below, from_above), (total, extra))
    state[...] = (total[...] + extra[...]).astype(state.dtype)
    line_products(state, line_tiles.at[0, 0], line_from, line_live, terms, products, sent)
    wait_sent(products, terms, sent)


def last_kernel(ids, line_got, local, zeros, from_below, from_above, running, out, total, extra, final, sent):
    collect(ids, line_got, (from_below, from_above), (total, extra))
    copies = [pltpu.make_async_copy(final.at[block], out.at[block], sent) for block in range(out.shape[0])]
    for block, copy in enumerate(copies):
        newest = (total[block] + extra[block]).astype(jnp.bfloat16).T.astype(jnp.float32)
        final[block] = (running[block] + newest) * (1.0 / (LAYERS + 1))
        copy.start()
    wait_sent(final, out, sent)


def on_device(
    grad_final, local_tiles, local_source, near_tiles, near_source, near_target,
    line_tiles, line_source, line_target, line_live,
):
    blocks, per_block, rows, cols = local_tiles.shape
    emb = grad_final.shape[1]
    slots = line_tiles.shape[2]
    nears = near_tiles.shape[2]
    bf16, f32 = jnp.bfloat16, jnp.float32
    dma = pltpu.SemaphoreType.DMA
    grad = grad_final.reshape(blocks, rows, emb)
    state_shape = pltpu.VMEM((blocks, emb, rows), bf16)
    sum_shape = pltpu.VMEM((blocks, emb, rows), f32)

    def emitted(extra):
        terms = (slots, emb + extra, cols)
        return (state_shape, pltpu.HBM(terms, bf16)), (VMEM, HBM), [pltpu.VMEM(terms, bf16), dma]

    shapes, specs, staging = emitted(ID_ROWS)
    indices = (line_source, line_live, near_source, near_target, local_source)
    state, terms, *indices = pl.pallas_call(
        first_kernel,
        out_shape=(*shapes, *(pltpu.SMEM(index.shape, jnp.int32) for index in indices)),
        in_specs=[HBM] * 8,
        out_specs=(*specs, *(SMEM for _ in indices)),
        scratch_shapes=[
            pltpu.VMEM((blocks, rows, emb), bf16),
            pltpu.VMEM((slots, rows, cols), bf16),
            pltpu.SMEM(line_target.shape, jnp.int32),
            *staging,
            dma((2,)),
            dma((6,)),
        ],
        compiler_params=PARAMS,
        name="first_terms",
    )(*off_chip(grad, line_tiles, line_source, line_live, line_target, near_source, near_target, local_source))
    line_source, line_live, near_source, near_target, local_source = in_scalars(*indices)
    (local_tiles,) = off_chip(local_tiles)
    line_tiles, near_tiles = on_chip(line_tiles, near_tiles)
    states, ids = [state], None
    for layer in range(LAYERS):
        first, last = layer == 0, layer == LAYERS - 1
        line_got = lax.all_to_all(terms, "blk", split_axis=0, concat_axis=0, tiled=True)
        near_shape = pltpu.VMEM((emb + ID_ROWS * first, cols), bf16)
        (state,) = on_chip(state)
        near_down, near_up = pl.pallas_call(
            functools.partial(near_kernel, with_ids=first),
            out_shape=(near_shape, near_shape),
            in_specs=[VMEM] * 2 + [SMEM] * 2,
            out_specs=(VMEM, VMEM),
            compiler_params=PARAMS,
            name="near_terms",
        )(state, near_tiles, near_source, near_target)
        local, zeros, *running = pl.pallas_call(
            functools.partial(local_kernel, last=last),
            out_shape=(sum_shape, sum_shape) + (pltpu.VMEM((blocks, rows, emb), f32),) * last,
            in_specs=[VMEM, HBM, SMEM] + [VMEM] * (2 * last),
            out_specs=(VMEM,) * (2 + last),
            scratch_shapes=[
                pltpu.VMEM(local_tiles.shape, bf16), dma((blocks,)),
            ],
            compiler_params=PARAMS,
            name="local_sums",
        )(
            state, local_tiles, local_source,
            *((grad, states[1]) if last else ()),
        )
        from_below = shifted(near_up, "grp", 1)
        from_above = shifted(near_down, "grp", -1)
        collected = on_chip(line_got, local, zeros, from_below, from_above)
        if not last:
            shapes, specs, staging = emitted(0)
            shapes += (sum_shape, sum_shape) + (pltpu.SMEM((slots + nears,), jnp.int32),) * first
            specs += (VMEM, VMEM) + (SMEM,) * first
            state, terms, _, _, *new_ids = pl.pallas_call(
                functools.partial(next_kernel, first=first),
                out_shape=shapes,
                in_specs=[SMEM] * (not first) + [VMEM] * 6 + [SMEM] * 2,
                out_specs=specs,
                scratch_shapes=staging,
                input_output_aliases={2 - first: 2, 3 - first: 3},
                compiler_params=PARAMS,
                name="next_state",
            )(*(() if first else (ids,)), *collected, line_tiles, line_source, line_live)
            if first:
                (ids,) = in_scalars(*new_ids)
            states.append(state)
        else:
            out, _, _ = pl.pallas_call(
                last_kernel,
                out_shape=(pltpu.HBM((blocks, rows, emb), f32), sum_shape, sum_shape),
                in_specs=[SMEM] + [VMEM] * 6,
                out_specs=(HBM, VMEM, VMEM),
                input_output_aliases={2: 1, 3: 2},
                scratch_shapes=[pltpu.VMEM((blocks, rows, emb), f32), dma],
                compiler_params=PARAMS,
                name="last_state",
            )(ids, *collected, *running)
    return out.reshape(blocks * rows, emb)


def solution(mesh):
    return jax.shard_map(
        on_device,
        mesh=mesh,
        in_specs=(
            P(("grp", "blk"), None),
            P(("grp", "blk"), None, None, None),
            P(("grp", "blk"), None),
            P("grp", "blk", None, None, None),
            P("grp", "blk", None),
            P("grp", "blk", None),
            P("grp", "blk", None, None, None),
            P("grp", "blk", None),
            P("grp", "blk", None),
            P("grp", "blk", None),
        ),
        out_specs=P(("grp", "blk"), None),
        check_vma=False,
    )
```
